32 devices in a mesh: track: 8 (over y, x, core), cols: 4 (over z).
Axes of the slice: x: 2, y: 2, z: 4, core: 2. Of those that a mesh axis runs over, the one named last changes fastest.
Arguments:
- design: bfloat16 [4096, 4096], P('track', 'cols'), may hold values from -0.09375 to 0.09375
- seg_start: int32 [4096], P('track'), may hold values from 0 to 4095, as said below
- seg_table: int32 [4096], P('track'), may hold values from 0 to 7, as said below
- taps: bfloat16 [8, 97], replicated, may hold values from -1.25 to 1.25
- ridge: float32 [4096], replicated, may hold values from 0.3 to 3
- col_perm: int32 [4096], replicated, may hold values from 0 to 4095, each once
Outputs:
- normals: float32 [4096, 4096], P('track', 'cols')
- factor: float32 [4096, 1024], P('track', 'cols')
The draws below stay inside these ranges and needn't reach their ends.
Inputs may be any that keep to these rules, and one draw needn't show every extreme that they name: seg_start[r] is the first row of the run of consecutive rows that holds row r; it never exceeds r, row 0 starts a run, the last row starts a run of its own, and all rows of a run carry the same value. `seg_table`: all rows with the same seg_start carry the same table. `col_perm`: each of 0 to 4095 once.
All inputs are finite; a program needn't handle non-finite values.
Results may differ from the reference program's by a relative error of at most 0.0019.
Values may be sent and summed in bfloat16 or wider, within the bound.
A program may use at most 64 MiB of HBM per device.

```python
import math
import jax
import jax.numpy as jnp
from jax import lax

SLAB = 4096
PANEL = 1024
TAPS = 97
TABLES = 8
ROW_DEV = 512
ROWS = 4096


def segment_layout(key):
    marks = jax.random.randint(jax.random.fold_in(key, 11), (ROWS,), 0, max(ROW_DEV // 8, 2))
    places = jnp.arange(ROWS, dtype=jnp.int32)
    begins = jnp.where((marks == 0) | (places == 0) | (places == ROWS - 1), places, 0)
    firsts = lax.cummax(begins)
    tables = jax.random.randint(jax.random.fold_in(key, 12), (ROWS,), 0, TABLES)
    return (firsts.astype(jnp.int32), jnp.take(tables, firsts).astype(jnp.int32))


def draw_seg_start(key, part):
    return segment_layout(key)[0]


def draw_seg_table(key, part):
    return segment_layout(key)[1]


def block_levels(stream_key, extent, cuts, smallest, high):
    def one(position, parts):
        steps = jax.random.uniform(jax.random.fold_in(jax.random.fold_in(stream_key, 6), position), (parts,), jnp.float32, smallest / len(cuts), high / len(cuts))
        return jnp.repeat(jnp.exp(steps), extent[position] // parts).reshape((-1,) + (1,) * (len(extent) - position - 1))

    factor_of = one(*cuts[0])
    for cut in cuts[1:]:
        factor_of = factor_of * one(*cut)
    return factor_of


def centred(rng, dims, scale, bound, cuts=(), kind=jnp.bfloat16):
    result = scale * jax.random.normal(rng, dims, jnp.float32)
    if cuts:
        result = result * block_levels(rng, dims, cuts, -0.22, 0.18)
    return jnp.clip(result, -bound, bound).astype(kind)


def setup_inputs(seed: int = 0) -> dict:
    splits = jax.random.split(jax.random.key(seed), 7)
    design = centred(splits[0], (ROWS, SLAB), ROWS ** -0.5, 0.09375, ((0, 8), (1, 4)))
    seg_start = draw_seg_start(jax.random.fold_in(splits[6], 71), 0)
    seg_table = draw_seg_table(jax.random.fold_in(splits[6], 71), 0)
    taps = centred(splits[3], (TABLES, TAPS), (TAPS // 4) ** -0.5, 1.25)
    ridge = jnp.clip(jnp.exp(jax.random.uniform(splits[4], (SLAB,), jnp.float32, math.log(0.3), math.log(3.0))), 0.3, 3.0)
    col_perm = jax.random.permutation(splits[5], SLAB).astype(jnp.int32)
    return dict(design=design, seg_start=seg_start, seg_table=seg_table, taps=taps, ridge=ridge, col_perm=col_perm)


def filter_rows(local, ext_top, seg_start, seg_table, taps, first_row):
    halo_rows = taps.shape[1] - 1
    row_count, columns = local.shape
    block = min(512, row_count)
    blocks = row_count // block
    extended = jnp.concatenate([ext_top, local], axis=0)
    upper = extended[:row_count].reshape(blocks, block, columns)
    lower_part = local.reshape(blocks, block, columns)[:, block - halo_rows:, :]
    windows = jnp.concatenate([upper, lower_part], axis=1)
    onehot = (seg_table[:, None] == jnp.arange(taps.shape[0], dtype=jnp.int32)[None, :]).astype(jnp.float32)
    row_taps = jnp.dot(onehot, taps.astype(jnp.float32), precision=lax.Precision.HIGHEST)
    flipped = row_taps[:, ::-1].reshape(blocks, block, halo_rows + 1)
    span = block + halo_rows
    padded = jnp.pad(flipped, ((0, 0), (0, 0), (0, span - halo_rows)))
    skewed = padded.reshape(blocks, block * (span + 1))[:, :block * span].reshape(blocks, block, span)
    offsets = (jnp.arange(blocks, dtype=jnp.int32) * block)[:, None, None]
    col_rows = first_row + offsets - halo_rows + jnp.arange(span, dtype=jnp.int32)[None, None, :]
    starts = seg_start.reshape(blocks, block)[:, :, None]
    coefs = jnp.where(col_rows >= starts, skewed, 0.0)
    summed = jnp.einsum('brj,bjc->brc', coefs, windows.astype(jnp.float32), precision=lax.Precision.HIGHEST)
    return summed.reshape(row_count, columns).astype(jnp.bfloat16)

def reference(design, seg_start, seg_table, taps, ridge, col_perm):
    ext_top = jnp.zeros((taps.shape[1] - 1, design.shape[1]), jnp.bfloat16)
    filtered = filter_rows(design, ext_top, seg_start, seg_table, taps, 0)
    normals = jnp.dot(filtered.T.astype(jnp.float32), filtered.astype(jnp.float32), preferred_element_type=jnp.float32) + jnp.diag(ridge)
    panel_ids = col_perm[:PANEL]
    panel_cols = jnp.take(normals, panel_ids, axis=1)
    panel_block = jnp.take(panel_cols, panel_ids, axis=0)
    lower = jnp.linalg.cholesky(panel_block)
    factor = lax.linalg.triangular_solve(lower, panel_cols, left_side=False, lower=True, transpose_a=True)
    return (normals, factor)
```

```python
import jax
import jax.numpy as jnp
from jax import lax
from jax.experimental import pallas as pl
from jax.experimental.pallas import tpu as pltpu
from jax.sharding import PartitionSpec as P

PANEL = 1024
TILE = 128
SUB = 8


def shifted(shard, axis, by):
    devices = lax.axis_size(axis)
    pairs = [(i, i + by) for i in range(devices) if 0 <= i + by < devices]
    return lax.ppermute(shard, axis, pairs)


def filter_rows(local, ext_top, seg_start, seg_table, taps, first_row):
    halo_rows = taps.shape[1] - 1
    row_count, columns = local.shape
    block = min(512, row_count)
    blocks = row_count // block
    extended = jnp.concatenate([ext_top, local], axis=0)
    upper = extended[:row_count].reshape(blocks, block, columns)
    lower_part = local.reshape(blocks, block, columns)[:, block - halo_rows :, :]
    windows = jnp.concatenate([upper, lower_part], axis=1)
    onehot = (seg_table[:, None] == jnp.arange(taps.shape[0], dtype=jnp.int32)[None, :]).astype(
        jnp.float32
    )
    row_taps = jnp.dot(onehot, taps.astype(jnp.float32), precision=lax.Precision.HIGHEST)
    flipped = row_taps[:, ::-1].reshape(blocks, block, halo_rows + 1)
    span = block + halo_rows
    padded = jnp.pad(flipped, ((0, 0), (0, 0), (0, span - halo_rows)))
    skewed = padded.reshape(blocks, block * (span + 1))[:, : block * span].reshape(
        blocks, block, span
    )
    offsets = (jnp.arange(blocks, dtype=jnp.int32) * block)[:, None, None]
    col_rows = first_row + offsets - halo_rows + jnp.arange(span, dtype=jnp.int32)[None, None, :]
    starts = seg_start.reshape(blocks, block)[:, :, None]
    coefs = jnp.where(col_rows >= starts, skewed, 0.0).astype(jnp.bfloat16)
    summed = jnp.einsum("brj,bjc->brc", coefs, windows, preferred_element_type=jnp.float32)
    return summed.reshape(row_count, columns).astype(jnp.bfloat16)


def split(x):
    hi = x.astype(jnp.bfloat16)
    lo = (x - hi.astype(jnp.float32)).astype(jnp.bfloat16)
    return hi, lo


def dot_nt(a, b):
    a_hi, a_lo = a
    b_hi, b_lo = b
    return lax.dot_general(
        jnp.concatenate([a_hi, a_hi, a_lo], axis=1),
        jnp.concatenate([b_hi, b_lo, b_hi], axis=1),
        (((1,), (1,)), ((), ())),
        preferred_element_type=jnp.float32,
    )


def tile_inverse_factor(work, linv):
    lane_shape = (SUB, TILE)
    sub_id = lax.broadcasted_iota(jnp.int32, lane_shape, 0)
    for g in range(TILE // SUB):
        base = g * SUB
        rows = work[base : base + SUB, :]
        left, right = rows[:, :TILE], rows[:, TILE:]
        cols = [
            jnp.broadcast_to(left[:, base + k : base + k + 1], lane_shape) for k in range(SUB)
        ]
        s = [
            [jnp.broadcast_to(cols[k][i : i + 1, :], lane_shape) for k in range(i + 1)]
            for i in range(SUB)
        ]
        inv_diag = []
        for k in range(SUB):
            r = lax.rsqrt(s[k][k])
            inv_diag.append(r)
            for i in range(k + 1, SUB):
                s[i][k] = s[i][k] * r
            for i in range(k + 1, SUB):
                for j in range(k + 1, i + 1):
                    s[i][j] = s[i][j] - s[i][k] * s[j][k]
        x = [[None] * SUB for _ in range(SUB)]
        for j in range(SUB):
            x[j][j] = inv_diag[j]
            for i in range(j + 1, SUB):
                total = s[i][j] * x[j][j]
                for m in range(j + 1, i):
                    total = total + s[i][m] * x[m][j]
                x[i][j] = -inv_diag[i] * total
        new_left = new_right = None
        for k in range(SUB):
            col = jnp.zeros(lane_shape, jnp.float32)
            for i in range(k, SUB):
                col = jnp.where(sub_id == i, x[i][k], col)
            term_l = col * jnp.broadcast_to(left[k : k + 1, :], lane_shape)
            term_r = col * jnp.broadcast_to(right[k : k + 1, :], lane_shape)
            new_left = term_l if new_left is None else new_left + term_l
            new_right = term_r if new_right is None else new_right + term_r
        linv[base : base + SUB, :] = new_right
        rest = base + SUB
        if rest < TILE:
            both = jnp.concatenate([new_left, new_right], axis=1)
            hi = both.astype(jnp.bfloat16).astype(jnp.float32)
            lo = both - hi
            pad = jnp.zeros_like(hi)
            lhs = jnp.concatenate(
                [hi[:, :TILE], hi[:, :TILE], lo[:, :TILE], pad[:, :TILE]], axis=0
            ).astype(jnp.bfloat16)
            rhs = jnp.concatenate([hi, lo, hi, pad], axis=0).astype(jnp.bfloat16)
            update = lax.dot_general(
                lhs, rhs, (((0,), (0,)), ((), ())), preferred_element_type=jnp.float32
            )
            work[rest:, :] = work[rest:, :] - update[rest:, :]


def factor_kernel(a_ref, out_ref, held, work, linv):
    size = a_ref.shape[0]
    tiles = size // TILE
    for j in range(tiles):
        held[j] = a_ref[:, j * TILE : (j + 1) * TILE]
    row = lax.broadcasted_iota(jnp.int32, (TILE, TILE), 0)
    lane = lax.broadcasted_iota(jnp.int32, (TILE, TILE), 1)
    eye = (row == lane).astype(jnp.float32)
    all_rows = lax.broadcasted_iota(jnp.int32, (size, TILE), 0)

    def step(k, carry):
        here = pl.ds(pl.multiple_of(k * TILE, TILE), TILE)
        work[:, :TILE] = held[k, here, :]
        work[:, TILE:] = eye
        tile_inverse_factor(work, linv)
        held[k, here, :] = eye
        column = dot_nt(split(held[k]), split(linv[...]))
        held[k] = column
        out_ref[:, here] = jnp.where(all_rows < (k + 1) * TILE, column, 0.0)
        parts = split(column)

        def update(j, inner):
            there = pl.ds(pl.multiple_of(j * TILE, TILE), TILE)
            other = split(held[k, there, :])
            held[j, here, :] = jnp.zeros((TILE, TILE), jnp.float32)
            held[j] = held[j] - dot_nt(parts, other)
            return inner

        lax.fori_loop(k + 1, tiles, update, 0)
        return carry

    lax.fori_loop(0, tiles, step, 0)


def inverse_factor_transposed(block, interpret=False):
    size = block.shape[0]
    return pl.pallas_call(
        factor_kernel,
        out_shape=jax.ShapeDtypeStruct((size, size), jnp.float32),
        in_specs=[pl.BlockSpec(memory_space=pltpu.VMEM)],
        out_specs=pl.BlockSpec(memory_space=pltpu.VMEM),
        scratch_shapes=[
            pltpu.VMEM((size // TILE, size, TILE), jnp.float32),
            pltpu.VMEM((TILE, 2 * TILE), jnp.float32),
            pltpu.VMEM((TILE, TILE), jnp.float32),
        ],
        compiler_params=pltpu.CompilerParams(vmem_limit_bytes=40 * 1024 * 1024),
        cost_estimate=pl.CostEstimate(
            flops=60_000_000_000, bytes_accessed=8 * size * size, transcendentals=size
        ),
        interpret=interpret,
    )(block)


def body(design, seg_start, seg_table, taps, ridge, col_perm):
    row_count, width_dev = design.shape
    halo_rows = taps.shape[1] - 1
    track_size = lax.axis_size("track")
    cols_size = lax.axis_size("cols")
    track_index = lax.axis_index("track")
    col_index = lax.axis_index("cols")
    ext_top = shifted(design[row_count - halo_rows :], "track", 1)
    filtered = filter_rows(design, ext_top, seg_start, seg_table, taps, track_index * row_count)
    gathered = lax.all_gather(filtered, "cols", axis=1, tiled=True)
    slab = gathered.shape[1]
    row_blk = slab // track_size
    panel_blk = PANEL // cols_size
    panel_ids = col_perm[:PANEL]
    own_ids = lax.dynamic_slice_in_dim(panel_ids, col_index * panel_blk, panel_blk)

    chosen = (jnp.arange(slab, dtype=jnp.int32)[:, None] == panel_ids[None, :]).astype(jnp.bfloat16)
    panel_filtered = jnp.dot(gathered, chosen, preferred_element_type=jnp.float32).astype(
        jnp.bfloat16
    )
    own_filtered = lax.dynamic_slice_in_dim(panel_filtered, col_index * panel_blk, panel_blk, 1)
    contract = (((0,), (0,)), ((), ()))

    part = lax.dot_general(
        panel_filtered, own_filtered, contract, preferred_element_type=jnp.float32
    )
    piece = lax.psum_scatter(part, "track", scatter_dimension=0, tiled=True)
    pieces = lax.all_gather(piece, ("track", "cols"), axis=0)
    block = (
        pieces.reshape(track_size, cols_size, PANEL // track_size, panel_blk)
        .transpose(0, 2, 1, 3)
        .reshape(PANEL, PANEL)
    )
    panel_ridge = jnp.take(ridge, panel_ids)
    ids = jnp.arange(PANEL, dtype=jnp.int32)
    block = block + jnp.where(ids[:, None] == ids[None, :], panel_ridge[:, None], 0.0)

    gathered, filtered, own_filtered, block = lax.optimization_barrier(
        (gathered, filtered, own_filtered, block)
    )
    inverse_t = inverse_factor_transposed(block)
    row_ids = track_index * row_blk + jnp.arange(row_blk, dtype=jnp.int32)
    row_ridge = lax.dynamic_slice_in_dim(ridge, track_index * row_blk, row_blk)

    own_part = lax.dot_general(gathered, own_filtered, contract, preferred_element_type=jnp.float32)
    own_cols = lax.psum_scatter(own_part, "track", scatter_dimension=0, tiled=True)
    own_cols = own_cols + jnp.where(row_ids[:, None] == own_ids[None, :], row_ridge[:, None], 0.0)
    panel_rows = lax.all_gather(own_cols, "cols", axis=1, tiled=True)

    sums = lax.psum_scatter(
        lax.dot_general(gathered, filtered, contract, preferred_element_type=jnp.float32),
        "track",
        scatter_dimension=0,
        tiled=True,
    )
    col_ids = col_index * width_dev + jnp.arange(width_dev, dtype=jnp.int32)
    normals = sums + jnp.where(row_ids[:, None] == col_ids[None, :], row_ridge[:, None], 0.0)

    own_inverse = lax.dynamic_slice_in_dim(inverse_t, col_index * panel_blk, panel_blk, 1)
    factor = jnp.dot(panel_rows, own_inverse, precision=lax.Precision.HIGHEST)
    return (normals, factor)


def solution(mesh):
    in_specs = (P("track", "cols"), P("track"), P("track"), P(), P(), P())
    out_specs = (P("track", "cols"), P("track", "cols"))
    return jax.shard_map(body, mesh=mesh, in_specs=in_specs, out_specs=out_specs, check_vma=False)
```

```python
import jax
import jax.numpy as jnp
from jax import lax
from jax.experimental import pallas as pl
from jax.experimental.pallas import tpu as pltpu
from jax.sharding import PartitionSpec as P

PANEL = 1024
TILE = 128
SUB = 8


def shifted(shard, axis, by):
    devices = lax.axis_size(axis)
    pairs = [(i, i + by) for i in range(devices) if 0 <= i + by < devices]
    return lax.ppermute(shard, axis, pairs)


def filter_rows(local, ext_top, seg_start, seg_table, taps, first_row):
    halo_rows = taps.shape[1] - 1
    row_count, columns = local.shape
    block = min(512, row_count)
    blocks = row_count // block
    extended = jnp.concatenate([ext_top, local], axis=0)
    upper = extended[:row_count].reshape(blocks, block, columns)
    lower_part = local.reshape(blocks, block, columns)[:, block - halo_rows :, :]
    windows = jnp.concatenate([upper, lower_part], axis=1)
    onehot = (seg_table[:, None] == jnp.arange(taps.shape[0], dtype=jnp.int32)[None, :]).astype(
        jnp.float32
    )
    row_taps = jnp.dot(onehot, taps.astype(jnp.float32), precision=lax.Precision.HIGHEST)
    flipped = row_taps[:, ::-1].reshape(blocks, block, halo_rows + 1)
    span = block + halo_rows
    padded = jnp.pad(flipped, ((0, 0), (0, 0), (0, span - halo_rows)))
    skewed = padded.reshape(blocks, block * (span + 1))[:, : block * span].reshape(
        blocks, block, span
    )
    offsets = (jnp.arange(blocks, dtype=jnp.int32) * block)[:, None, None]
    col_rows = first_row + offsets - halo_rows + jnp.arange(span, dtype=jnp.int32)[None, None, :]
    starts = seg_start.reshape(blocks, block)[:, :, None]
    coefs = jnp.where(col_rows >= starts, skewed, 0.0).astype(jnp.bfloat16)
    summed = jnp.einsum("brj,bjc->brc", coefs, windows, preferred_element_type=jnp.float32)
    return summed.reshape(row_count, columns).astype(jnp.bfloat16)


def split(x):
    hi = x.astype(jnp.bfloat16)
    lo = (x - hi.astype(jnp.float32)).astype(jnp.bfloat16)
    return hi, lo


def dot_nt(a, b):
    a_hi, a_lo = a
    b_hi, b_lo = b
    return lax.dot_general(
        jnp.concatenate([a_hi, a_hi, a_lo], axis=1),
        jnp.concatenate([b_hi, b_lo, b_hi], axis=1),
        (((1,), (1,)), ((), ())),
        preferred_element_type=jnp.float32,
    )


def tile_inverse_factor(work, linv):
    lane_shape = (SUB, TILE)
    sub_id = lax.broadcasted_iota(jnp.int32, lane_shape, 0)
    for g in range(TILE // SUB):
        base = g * SUB
        rows = work[base : base + SUB, :]
        left, right = rows[:, :TILE], rows[:, TILE:]
        cols = [
            jnp.broadcast_to(left[:, base + k : base + k + 1], lane_shape) for k in range(SUB)
        ]
        s = [
            [jnp.broadcast_to(cols[k][i : i + 1, :], lane_shape) for k in range(i + 1)]
            for i in range(SUB)
        ]
        inv_diag = []
        for k in range(SUB):
            r = lax.rsqrt(s[k][k])
            inv_diag.append(r)
            for i in range(k + 1, SUB):
                s[i][k] = s[i][k] * r
            for i in range(k + 1, SUB):
                for j in range(k + 1, i + 1):
                    s[i][j] = s[i][j] - s[i][k] * s[j][k]
        x = [[None] * SUB for _ in range(SUB)]
        for j in range(SUB):
            x[j][j] = inv_diag[j]
            for i in range(j + 1, SUB):
                total = s[i][j] * x[j][j]
                for m in range(j + 1, i):
                    total = total + s[i][m] * x[m][j]
                x[i][j] = -inv_diag[i] * total
        new_left = new_right = None
        for k in range(SUB):
            col = jnp.zeros(lane_shape, jnp.float32)
            for i in range(k, SUB):
                col = jnp.where(sub_id == i, x[i][k], col)
            term_l = col * jnp.broadcast_to(left[k : k + 1, :], lane_shape)
            term_r = col * jnp.broadcast_to(right[k : k + 1, :], lane_shape)
            new_left = term_l if new_left is None else new_left + term_l
            new_right = term_r if new_right is None else new_right + term_r
        linv[base : base + SUB, :] = new_right
        rest = base + SUB
        if rest < TILE:
            both = jnp.concatenate([new_left, new_right], axis=1)
            hi = both.astype(jnp.bfloat16).astype(jnp.float32)
            lo = both - hi
            pad = jnp.zeros_like(hi)
            lhs = jnp.concatenate(
                [hi[:, :TILE], hi[:, :TILE], lo[:, :TILE], pad[:, :TILE]], axis=0
            ).astype(jnp.bfloat16)
            rhs = jnp.concatenate([hi, lo, hi, pad], axis=0).astype(jnp.bfloat16)
            update = lax.dot_general(
                lhs, rhs, (((0,), (0,)), ((), ())), preferred_element_type=jnp.float32
            )
            work[rest:, :] = work[rest:, :] - update[rest:, :]


def factor_kernel(a_ref, out_ref, held, work, linv):
    size = a_ref.shape[0]
    tiles = size // TILE
    for j in range(tiles):
        held[j] = a_ref[:, j * TILE : (j + 1) * TILE]
    row = lax.broadcasted_iota(jnp.int32, (TILE, TILE), 0)
    lane = lax.broadcasted_iota(jnp.int32, (TILE, TILE), 1)
    eye = (row == lane).astype(jnp.float32)
    all_rows = lax.broadcasted_iota(jnp.int32, (size, TILE), 0)

    def step(k, carry):
        here = pl.ds(pl.multiple_of(k * TILE, TILE), TILE)
        work[:, :TILE] = held[k, here, :]
        work[:, TILE:] = eye
        tile_inverse_factor(work, linv)
        held[k, here, :] = eye
        column = dot_nt(split(held[k]), split(linv[...]))
        held[k] = column
        out_ref[:, here] = jnp.where(all_rows < (k + 1) * TILE, column, 0.0)
        parts = split(column)

        def update(j, inner):
            there = pl.ds(pl.multiple_of(j * TILE, TILE), TILE)
            other = split(held[k, there, :])
            held[j, here, :] = jnp.zeros((TILE, TILE), jnp.float32)
            held[j] = held[j] - dot_nt(parts, other)
            return inner

        lax.fori_loop(k + 1, tiles, update, 0)
        return carry

    lax.fori_loop(0, tiles, step, 0)


def inverse_factor_transposed(block, interpret=False):
    size = block.shape[0]
    return pl.pallas_call(
        factor_kernel,
        out_shape=jax.ShapeDtypeStruct((size, size), jnp.float32),
        in_specs=[pl.BlockSpec(memory_space=pltpu.VMEM)],
        out_specs=pl.BlockSpec(memory_space=pltpu.VMEM),
        scratch_shapes=[
            pltpu.VMEM((size // TILE, size, TILE), jnp.float32),
            pltpu.VMEM((TILE, 2 * TILE), jnp.float32),
            pltpu.VMEM((TILE, TILE), jnp.float32),
        ],
        compiler_params=pltpu.CompilerParams(vmem_limit_bytes=40 * 1024 * 1024),
        cost_estimate=pl.CostEstimate(
            flops=60_000_000_000, bytes_accessed=8 * size * size, transcendentals=size
        ),
        interpret=interpret,
    )(block)


def body(design, seg_start, seg_table, taps, ridge, col_perm):
    row_count, width_dev = design.shape
    halo_rows = taps.shape[1] - 1
    track_index = lax.axis_index("track")
    col_index = lax.axis_index("cols")
    ext_top = shifted(design[row_count - halo_rows :], "track", 1)
    filtered = filter_rows(design, ext_top, seg_start, seg_table, taps, track_index * row_count)
    gathered = lax.all_gather(filtered, "cols", axis=1, tiled=True)
    slab = gathered.shape[1]
    row_blk = slab // lax.axis_size("track")
    panel_blk = PANEL // lax.axis_size("cols")
    panel_ids = col_perm[:PANEL]

    chosen = (jnp.arange(slab, dtype=jnp.int32)[:, None] == panel_ids[None, :]).astype(jnp.bfloat16)
    panel_filtered = jnp.dot(gathered, chosen, preferred_element_type=jnp.float32).astype(
        jnp.bfloat16
    )
    contract = (((0,), (0,)), ((), ()))

    panel_all = lax.all_gather(panel_filtered, "track", axis=0, tiled=True)
    rows_all = lax.all_to_all(gathered, "track", split_axis=1, concat_axis=0, tiled=True)
    filtered, panel_all, rows_all = lax.optimization_barrier((filtered, panel_all, rows_all))
    cols_all = lax.all_gather(filtered, "track", axis=0, tiled=True)

    block = lax.dot_general(panel_all, panel_all, contract, preferred_element_type=jnp.float32)
    panel_ridge = jnp.take(ridge, panel_ids)
    ids = jnp.arange(PANEL, dtype=jnp.int32)
    block = block + jnp.where(ids[:, None] == ids[None, :], panel_ridge[:, None], 0.0)
    inverse_t = inverse_factor_transposed(block)

    row_ids = track_index * row_blk + jnp.arange(row_blk, dtype=jnp.int32)
    row_ridge = lax.dynamic_slice_in_dim(ridge, track_index * row_blk, row_blk)
    panel_rows = lax.dot_general(rows_all, panel_all, contract, preferred_element_type=jnp.float32)
    panel_rows = panel_rows + jnp.where(
        row_ids[:, None] == panel_ids[None, :], row_ridge[:, None], 0.0
    )
    own_inverse = lax.dynamic_slice_in_dim(inverse_t, col_index * panel_blk, panel_blk, 1)
    factor = jnp.dot(panel_rows, own_inverse, precision=lax.Precision.HIGHEST)

    sums = lax.dot_general(rows_all, cols_all, contract, preferred_element_type=jnp.float32)
    col_ids = col_index * width_dev + jnp.arange(width_dev, dtype=jnp.int32)
    normals = sums + jnp.where(row_ids[:, None] == col_ids[None, :], row_ridge[:, None], 0.0)
    return (normals, factor)


def solution(mesh):
    in_specs = (P("track", "cols"), P("track"), P("track"), P(), P(), P())
    out_specs = (P("track", "cols"), P("track", "cols"))
    return jax.shard_map(body, mesh=mesh, in_specs=in_specs, out_specs=out_specs, check_vma=False)
```

```python
import jax
import jax.numpy as jnp
from jax import lax
from jax.experimental import pallas as pl
from jax.experimental.pallas import tpu as pltpu
from jax.sharding import PartitionSpec as P

PANEL = 1024
TILE = 128
SUB = 8


def shifted(shard, axis, by):
    devices = lax.axis_size(axis)
    pairs = [(i, i + by) for i in range(devices) if 0 <= i + by < devices]
    return lax.ppermute(shard, axis, pairs)


def filter_rows(local, ext_top, seg_start, seg_table, taps, first_row):
    halo_rows = taps.shape[1] - 1
    row_count, columns = local.shape
    block = min(512, row_count)
    blocks = row_count // block
    extended = jnp.concatenate([ext_top, local], axis=0)
    upper = extended[:row_count].reshape(blocks, block, columns)
    lower_part = local.reshape(blocks, block, columns)[:, block - halo_rows :, :]
    windows = jnp.concatenate([upper, lower_part], axis=1)
    onehot = (seg_table[:, None] == jnp.arange(taps.shape[0], dtype=jnp.int32)[None, :]).astype(
        jnp.float32
    )
    row_taps = jnp.dot(onehot, taps.astype(jnp.float32), precision=lax.Precision.HIGHEST)
    flipped = row_taps[:, ::-1].reshape(blocks, block, halo_rows + 1)
    span = block + halo_rows
    padded = jnp.pad(flipped, ((0, 0), (0, 0), (0, span - halo_rows)))
    skewed = padded.reshape(blocks, block * (span + 1))[:, : block * span].reshape(
        blocks, block, span
    )
    offsets = (jnp.arange(blocks, dtype=jnp.int32) * block)[:, None, None]
    col_rows = first_row + offsets - halo_rows + jnp.arange(span, dtype=jnp.int32)[None, None, :]
    starts = seg_start.reshape(blocks, block)[:, :, None]
    coefs = jnp.where(col_rows >= starts, skewed, 0.0).astype(jnp.bfloat16)
    summed = jnp.einsum("brj,bjc->brc", coefs, windows, preferred_element_type=jnp.float32)
    return summed.reshape(row_count, columns).astype(jnp.bfloat16)


def exchanged(part_for, own, axis):
    devices = lax.axis_size(axis)
    index = lax.axis_index(axis)
    out = [own]
    for d in range(1, devices):
        pairs = [(i, (i + d) % devices) for i in range(devices)]
        out.append(lax.ppermute(part_for((index + d) % devices), axis, pairs))
    return out


def in_order(parts, axis):
    devices = lax.axis_size(axis)
    index = lax.axis_index(axis)
    rows = parts[0].shape[0]
    whole = jnp.zeros((devices * rows, parts[0].shape[1]), parts[0].dtype)
    for d, part in enumerate(parts):
        whole = lax.dynamic_update_slice_in_dim(
            whole, part, ((index - d) % devices) * rows, 0
        )
    return whole


def split(x):
    hi = x.astype(jnp.bfloat16)
    lo = (x - hi.astype(jnp.float32)).astype(jnp.bfloat16)
    return hi, lo


def dot_nt(a, b):
    a_hi, a_lo = a
    b_hi, b_lo = b
    return lax.dot_general(
        jnp.concatenate([a_hi, a_hi, a_lo], axis=1),
        jnp.concatenate([b_hi, b_lo, b_hi], axis=1),
        (((1,), (1,)), ((), ())),
        preferred_element_type=jnp.float32,
    )


def tile_inverse_factor(work, linv):
    lane_shape = (SUB, TILE)
    sub_id = lax.broadcasted_iota(jnp.int32, lane_shape, 0)
    for g in range(TILE // SUB):
        base = g * SUB
        rows = work[base : base + SUB, :]
        left, right = rows[:, :TILE], rows[:, TILE:]
        cols = [
            jnp.broadcast_to(left[:, base + k : base + k + 1], lane_shape) for k in range(SUB)
        ]
        s = [
            [jnp.broadcast_to(cols[k][i : i + 1, :], lane_shape) for k in range(i + 1)]
            for i in range(SUB)
        ]
        inv_diag = []
        for k in range(SUB):
            r = lax.rsqrt(s[k][k])
            inv_diag.append(r)
            for i in range(k + 1, SUB):
                s[i][k] = s[i][k] * r
            for i in range(k + 1, SUB):
                for j in range(k + 1, i + 1):
                    s[i][j] = s[i][j] - s[i][k] * s[j][k]
        x = [[None] * SUB for _ in range(SUB)]
        for j in range(SUB):
            x[j][j] = inv_diag[j]
            for i in range(j + 1, SUB):
                total = s[i][j] * x[j][j]
                for m in range(j + 1, i):
                    total = total + s[i][m] * x[m][j]
                x[i][j] = -inv_diag[i] * total
        new_left = new_right = None
        for k in range(SUB):
            col = jnp.zeros(lane_shape, jnp.float32)
            for i in range(k, SUB):
                col = jnp.where(sub_id == i, x[i][k], col)
            term_l = col * jnp.broadcast_to(left[k : k + 1, :], lane_shape)
            term_r = col * jnp.broadcast_to(right[k : k + 1, :], lane_shape)
            new_left = term_l if new_left is None else new_left + term_l
            new_right = term_r if new_right is None else new_right + term_r
        linv[base : base + SUB, :] = new_right
        rest = base + SUB
        if rest < TILE:
            both = jnp.concatenate([new_left, new_right], axis=1)
            hi = both.astype(jnp.bfloat16).astype(jnp.float32)
            lo = both - hi
            pad = jnp.zeros_like(hi)
            lhs = jnp.concatenate(
                [hi[:, :TILE], hi[:, :TILE], lo[:, :TILE], pad[:, :TILE]], axis=0
            ).astype(jnp.bfloat16)
            rhs = jnp.concatenate([hi, lo, hi, pad], axis=0).astype(jnp.bfloat16)
            update = lax.dot_general(
                lhs, rhs, (((0,), (0,)), ((), ())), preferred_element_type=jnp.float32
            )
            work[rest:, :] = work[rest:, :] - update[rest:, :]


def factor_kernel(a_ref, out_ref, held, work, linv):
    size = a_ref.shape[0]
    tiles = size // TILE
    for j in range(tiles):
        held[j] = a_ref[:, j * TILE : (j + 1) * TILE]
    row = lax.broadcasted_iota(jnp.int32, (TILE, TILE), 0)
    lane = lax.broadcasted_iota(jnp.int32, (TILE, TILE), 1)
    eye = (row == lane).astype(jnp.float32)
    all_rows = lax.broadcasted_iota(jnp.int32, (size, TILE), 0)

    def step(k, carry):
        here = pl.ds(pl.multiple_of(k * TILE, TILE), TILE)
        work[:, :TILE] = held[k, here, :]
        work[:, TILE:] = eye
        tile_inverse_factor(work, linv)
        held[k, here, :] = eye
        column = dot_nt(split(held[k]), split(linv[...]))
        held[k] = column
        out_ref[:, here] = jnp.where(all_rows < (k + 1) * TILE, column, 0.0)
        parts = split(column)

        def update(j, inner):
            there = pl.ds(pl.multiple_of(j * TILE, TILE), TILE)
            other = split(held[k, there, :])
            held[j, here, :] = jnp.zeros((TILE, TILE), jnp.float32)
            held[j] = held[j] - dot_nt(parts, other)
            return inner

        lax.fori_loop(k + 1, tiles, update, 0)
        return carry

    lax.fori_loop(0, tiles, step, 0)


def inverse_factor_transposed(block, interpret=False):
    size = block.shape[0]
    return pl.pallas_call(
        factor_kernel,
        out_shape=jax.ShapeDtypeStruct((size, size), jnp.float32),
        in_specs=[pl.BlockSpec(memory_space=pltpu.VMEM)],
        out_specs=pl.BlockSpec(memory_space=pltpu.VMEM),
        scratch_shapes=[
            pltpu.VMEM((size // TILE, size, TILE), jnp.float32),
            pltpu.VMEM((TILE, 2 * TILE), jnp.float32),
            pltpu.VMEM((TILE, TILE), jnp.float32),
        ],
        compiler_params=pltpu.CompilerParams(vmem_limit_bytes=40 * 1024 * 1024),
        cost_estimate=pl.CostEstimate(
            flops=60_000_000_000, bytes_accessed=8 * size * size, transcendentals=size
        ),
        interpret=interpret,
    )(block)


def body(design, seg_start, seg_table, taps, ridge, col_perm):
    row_count, width_dev = design.shape
    halo_rows = taps.shape[1] - 1
    track_index = lax.axis_index("track")
    col_index = lax.axis_index("cols")
    ext_top = shifted(design[row_count - halo_rows :], "track", 1)
    filtered = filter_rows(design, ext_top, seg_start, seg_table, taps, track_index * row_count)
    gathered = lax.all_gather(filtered, "cols", axis=1, tiled=True)
    slab = gathered.shape[1]
    row_blk = slab // lax.axis_size("track")
    panel_blk = PANEL // lax.axis_size("cols")
    panel_ids = col_perm[:PANEL]

    chosen = (jnp.arange(slab, dtype=jnp.int32)[:, None] == panel_ids[None, :]).astype(jnp.bfloat16)
    panel_ridge = jnp.take(ridge, panel_ids)

    cols_all = exchanged(lambda d: filtered, filtered, "track")
    gathered, cols_all, panel_ridge = lax.optimization_barrier((gathered, cols_all, panel_ridge))

    panel_filtered = jnp.dot(gathered, chosen, preferred_element_type=jnp.float32).astype(
        jnp.bfloat16
    )
    contract = (((0,), (0,)), ((), ()))
    panel_all = lax.all_gather(panel_filtered, "track", axis=0, tiled=True)
    gathered, panel_all = lax.optimization_barrier((gathered, panel_all))

    block = lax.dot_general(panel_all, panel_all, contract, preferred_element_type=jnp.float32)
    ids = jnp.arange(PANEL, dtype=jnp.int32)
    block = block + jnp.where(ids[:, None] == ids[None, :], panel_ridge[:, None], 0.0)
    inverse_t = inverse_factor_transposed(block)

    def columns_of(device):
        return lax.dynamic_slice_in_dim(gathered, device * row_blk, row_blk, 1)

    rows_all = exchanged(columns_of, columns_of(track_index), "track")
    inverse_t, panel_all, *rows_all = lax.optimization_barrier((inverse_t, panel_all, *rows_all))
    rows_all = in_order(rows_all, "track")
    cols_all = in_order(cols_all, "track")

    row_ids = track_index * row_blk + jnp.arange(row_blk, dtype=jnp.int32)
    row_ridge = lax.dynamic_slice_in_dim(ridge, track_index * row_blk, row_blk)
    panel_rows = lax.dot_general(rows_all, panel_all, contract, preferred_element_type=jnp.float32)
    panel_rows = panel_rows + jnp.where(
        row_ids[:, None] == panel_ids[None, :], row_ridge[:, None], 0.0
    )
    own_inverse = lax.dynamic_slice_in_dim(inverse_t, col_index * panel_blk, panel_blk, 1)
    factor = jnp.dot(panel_rows, own_inverse, precision=lax.Precision.HIGHEST)

    sums = lax.dot_general(rows_all, cols_all, contract, preferred_element_type=jnp.float32)
    col_ids = col_index * width_dev + jnp.arange(width_dev, dtype=jnp.int32)
    normals = sums + jnp.where(row_ids[:, None] == col_ids[None, :], row_ridge[:, None], 0.0)
    return (normals, factor)


def solution(mesh):
    in_specs = (P("track", "cols"), P("track"), P("track"), P(), P(), P())
    out_specs = (P("track", "cols"), P("track", "cols"))
    return jax.shard_map(body, mesh=mesh, in_specs=in_specs, out_specs=out_specs, check_vma=False)
```
